128 devices in a mesh: rep: 4 (over x), ep: 32 (over y, z, core).
Axes of the slice: x: 4, y: 4, z: 4, core: 2. Of those that a mesh axis runs over, the one named last changes fastest.
Arguments:
- q_latent: bfloat16 [1024, 128, 512], P(('rep', 'ep')), may hold values from -6 to 6
- q_rope: bfloat16 [1024, 128, 64], P(('rep', 'ep')), may hold values from -104 to 104
- cache_latent: bfloat16 [1024, 128, 512], P(('rep', 'ep')), may hold values from -6 to 6
- cache_rope: bfloat16 [1024, 128, 64], P(('rep', 'ep')), may hold values from -6 to 6
- cache_len: int32 [1024], P(('rep', 'ep')), may hold values from 32 to 128, as said below
- stream: bfloat16 [1024, 7168], P(('rep', 'ep')), may hold values from -6 to 6
- norm_gain: float32 [7168], replicated, may hold values from 0.1 to 1.9
- expert_ids: int32 [1024, 8], P(('rep', 'ep')), may hold values from 0 to 63, all different within a row; in each aligned block of 8 rows (0 to 7, 8 to 15, ...) at most 2 rows name the same one
- route_weights: bfloat16 [1024, 8], P(('rep', 'ep')), may hold values from 0.099609375 to 1
- w_gate: bfloat16 [64, 7168, 1024], P('ep', None, 'rep'), may hold values from -0.0625 to 0.0625
- w_up: bfloat16 [64, 7168, 1024], P('ep', None, 'rep'), may hold values from -0.0625 to 0.0625
- w_down: bfloat16 [64, 1024, 7168], P('ep', 'rep'), may hold values from -0.1875 to 0.1875
Outputs:
- attn_latent: bfloat16 [1024, 128, 512], P(('rep', 'ep'))
- layer_out: bfloat16 [1024, 7168], P(('rep', 'ep'))
The draws below stay inside these ranges and needn't reach their ends.
Inputs may be any that keep to these rules, and one draw needn't show every extreme that they name: `expert_ids`: each row names 8 different experts; within the rows of one device no expert is named by more than 2 rows, a bound that some block reaches. `cache_len`: some row has all 128 positions live.
All inputs are finite; a program needn't handle non-finite values.
Results may differ from the reference program's by a relative error of at most 0.01.
Values may be sent and summed in bfloat16 or wider, within the bound.
No kernel may reach another device: no remote copies, remote signals or barrier semaphores. Data moves between devices by JAX's collectives and lax.ppermute only.
A program may use at most 128 MiB of HBM per device.

```python
import math
import jax
import jax.numpy as jnp
import numpy as np
from jax import lax

D = 7168
HEADS = 128
LATENT = 512
ROPE = 64
FF = 1024
TOP = 8
R_DEV = 8
CACHE = 128
EXPERTS = 64
ROWS = 1024
CAP = 2
N_REP = 4
N_EP = 32


def attention_draws(key):
    key_ql = jax.random.fold_in(key, 101)
    key_qr = jax.random.fold_in(key, 102)
    key_cl = jax.random.fold_in(key, 103)
    key_cr = jax.random.fold_in(key, 104)
    query_lat = jnp.clip(jax.random.normal(key_ql, (ROWS, HEADS, LATENT), jnp.float32), -6.0, 6.0)
    query_rot = jnp.clip(jax.random.normal(key_qr, (ROWS, HEADS, ROPE), jnp.float32), -6.0, 6.0)
    keys_lat = jnp.clip(jax.random.normal(key_cl, (ROWS, CACHE, LATENT), jnp.float32), -6.0, 6.0)
    keys_rot = jnp.clip(jax.random.normal(key_cr, (ROWS, CACHE, ROPE), jnp.float32), -6.0, 6.0)
    return (query_lat, query_rot, keys_lat, keys_rot)


def draw_q_latent(key, part):
    return attention_draws(key)[0].astype(jnp.bfloat16)


def draw_q_rope(key, part):
    return attention_draws(key)[1].astype(jnp.bfloat16)


def draw_cache_latent(key, part):
    return attention_draws(key)[2].astype(jnp.bfloat16)


def draw_cache_rope(key, part):
    return attention_draws(key)[3].astype(jnp.bfloat16)


def draw_cache_len(key, part):
    lengths = jax.random.randint(jax.random.fold_in(key, 201), (ROWS,), CACHE // 4, CACHE + 1, jnp.int32)
    return lengths.at[0].set(CACHE)


def levels(key, shape, shards, least, high):
    factor_of = 1.0
    for dim, blocks in shards:
        steps = jax.random.uniform(jax.random.fold_in(jax.random.fold_in(key, 6), dim), (blocks,), jnp.float32, least / len(shards), high / len(shards))
        factor_of = factor_of * jnp.repeat(jnp.exp(steps), shape[dim] // blocks).reshape((-1,) + (1,) * (len(shape) - 1 - dim))
    return factor_of


def shared_out(own_key, own, number, rows, count, top, reach, lean):
    order = jax.random.permutation(own_key, count)
    crowded, ordinary = load_shares(count, rows * top, reach, lean, True), load_shares(count, rows * top, reach, lean, False)
    places = jnp.arange(count)

    def named(tallies, turn):
        used = int((tallies > 0).sum())
        fixed = max(1, used // 4)
        shifted = fixed + (places - fixed + turn * (used - fixed)) % max(1, count - fixed)
        return jnp.zeros((count,), jnp.int32).at[order[jnp.where(places < fixed, places, shifted)]].set(jnp.asarray(tallies, jnp.int32))

    tallies = jnp.where(number % 4 == 0, named(crowded, number // 4), named(ordinary, number - number // 4 - 1))
    mixed = jax.random.permutation(jax.random.fold_in(own, 3), count)
    donor, receiver = mixed[0:count // 2 * 2:2], mixed[1:count // 2 * 2:2]
    slack = jnp.minimum(tallies[donor] - 1, reach - tallies[receiver]) // 2
    slack = jnp.where((donor == order[0]) | (receiver == order[0]) | (tallies[receiver] == 0), 0, jnp.maximum(slack, 0))
    shifted = jax.random.randint(jax.random.fold_in(own, 4), (count // 2,), 0, 1 << 20) % (slack + 1)
    tallies = tallies.at[donor].add(-shifted).at[receiver].add(shifted)
    items = jnp.searchsorted(jnp.cumsum(tallies), jnp.arange(rows * top), side="right").astype(jnp.int32)
    grid = items.reshape(top, rows).T
    grid = grid[jax.random.permutation(jax.random.fold_in(own, 1), rows)]
    turn = jax.random.randint(jax.random.fold_in(own, 2), (rows, 1), 0, top)
    return jnp.take_along_axis(grid, (jnp.arange(top)[None, :] + turn) % top, axis=1)


def load_shares(number_of, total, most, skew, full):
    loads = [(1 << 20) // math.isqrt(standing ** skew) + 1 for standing in range(1, number_of + 1)]
    largest = most if full else min(most, max(-(-total // number_of), total * loads[0] // sum(loads)))
    least = 1 if total - largest >= number_of - 1 else 0
    counts, spare = [largest] + [least] * (number_of - 1), total - largest - least * (number_of - 1)
    while spare > 0:
        movable = [i for i in range(1, number_of) if counts[i] < largest] or [i for i in range(1, number_of) if counts[i] < most]
        whole, remaining = sum([loads[i] for i in movable]), spare
        for i in movable:
            extra = min(most - counts[i], max(1, remaining * loads[i] // whole), spare)
            counts[i] = counts[i] + extra
            spare = spare - extra
    return np.array(counts)


def gaussian(stream_key, dims, scale, most, split=(), kind=jnp.bfloat16):
    level = levels(stream_key, dims, split, -0.22, 0.18) if split else 1.0
    array = jax.random.normal(stream_key, dims, jnp.float32) * scale * level
    return jnp.minimum(jnp.maximum(array, -most), most).astype(kind)


def setup_inputs(seed: int = 0) -> dict:
    key_list = jax.random.split(jax.random.key(seed), 13)
    q_latent = draw_q_latent(jax.random.fold_in(key_list[12], 71), 0)
    q_rope = draw_q_rope(jax.random.fold_in(key_list[12], 71), 0)
    cache_latent = draw_cache_latent(jax.random.fold_in(key_list[12], 71), 0)
    cache_rope = draw_cache_rope(jax.random.fold_in(key_list[12], 71), 0)
    cache_len = draw_cache_len(jax.random.fold_in(key_list[12], 71), 0)
    stream = gaussian(key_list[5], (ROWS, D), 1.0, 6.0, ((0, 128),))
    norm_gain = jnp.clip(1.0 + 0.18 * jax.random.normal(key_list[6], (D,), jnp.float32), 0.1, 1.9)
    expert_ids_keys = jax.random.split(jax.random.fold_in(key_list[7], 1), ROWS // R_DEV)
    expert_ids_turns = jax.random.permutation(jax.random.fold_in(key_list[7], 3), ROWS // R_DEV)
    expert_ids = jax.vmap(lambda own, number: shared_out(jax.random.fold_in(key_list[7], 2), own, number, R_DEV, EXPERTS, TOP, CAP, 2))(expert_ids_keys, expert_ids_turns).reshape((ROWS, TOP))
    route_weights = jnp.clip(0.099609375 + 0.9003906 * jax.random.uniform(key_list[8], (ROWS, TOP), jnp.float32) ** levels(key_list[8], (ROWS, TOP), ((0, 128),), -0.2, 0.2), 0.099609375, 1.0).astype(jnp.bfloat16)
    w_gate = gaussian(key_list[9], (EXPERTS, D, FF), D ** -0.5, 0.0625, ((0, 32), (2, 4)))
    w_up = gaussian(key_list[10], (EXPERTS, D, FF), D ** -0.5, 0.0625, ((0, 32), (2, 4)))
    w_down = gaussian(key_list[11], (EXPERTS, FF, D), FF ** -0.5, 0.1875, ((0, 32), (1, 4)))
    return {"q_latent": q_latent, "q_rope": q_rope, "cache_latent": cache_latent, "cache_rope": cache_rope, "cache_len": cache_len, "stream": stream, "norm_gain": norm_gain, "expert_ids": expert_ids, "route_weights": route_weights, "w_gate": w_gate, "w_up": w_up, "w_down": w_down}


score_scale = 192.0 ** (-0.5)
norm_eps = 1e-06

def attend_row(item):
    query_lat, query_rot, keys_lat, keys_rot, length = item
    scores = (jnp.einsum('hl,tl->ht', query_lat.astype(jnp.float32), keys_lat.astype(jnp.float32)) + jnp.einsum('hr,tr->ht', query_rot.astype(jnp.float32), keys_rot.astype(jnp.float32))) * score_scale
    valid_mask = (jnp.arange(CACHE, dtype=jnp.int32) < length)[None, :]
    scores = jnp.where(valid_mask, scores, -1e+30)
    top_score = lax.optimization_barrier(jnp.max(scores, axis=-1, keepdims=True))
    exponent = jnp.where(valid_mask, jnp.exp(scores - top_score), 0.0)
    attn_weights = (exponent / lax.optimization_barrier(jnp.sum(exponent, axis=-1, keepdims=True))).astype(jnp.bfloat16)
    return jnp.einsum('ht,tl->hl', attn_weights.astype(jnp.float32), keys_lat.astype(jnp.float32)).astype(jnp.bfloat16)

def reference(q_latent, q_rope, cache_latent, cache_rope, cache_len, stream, norm_gain, expert_ids, route_weights, w_gate, w_up, w_down):
    attn_latent = lax.map(attend_row, (q_latent, q_rope, cache_latent, cache_rope, cache_len))
    stream_f = stream.astype(jnp.float32)
    normed = (stream_f * lax.rsqrt(lax.optimization_barrier(jnp.mean(stream_f * stream_f, axis=-1, keepdims=True)) + norm_eps) * norm_gain).astype(jnp.bfloat16)
    assigned = expert_ids.reshape(-1)
    onehot = (assigned[:, None] == jnp.arange(EXPERTS, dtype=jnp.int32)[None, :]).astype(jnp.int32)
    earlier = jnp.cumsum(onehot, axis=0) - onehot
    position = lax.optimization_barrier(jnp.sum(earlier * onehot, axis=-1)).astype(jnp.int32)
    slot_limit = N_REP * N_EP * CAP
    row_of = (jnp.arange(ROWS * TOP, dtype=jnp.int32) // TOP).astype(jnp.int32)
    table = jnp.zeros((EXPERTS, slot_limit), jnp.int32).at[assigned, position].set(row_of)
    weight_table = jnp.zeros((EXPERTS, slot_limit), jnp.float32).at[assigned, position].set(route_weights.reshape(-1).astype(jnp.float32))
    block = FF // N_REP

    def expert_step(total, item):
        gate_mat, up_mat, down_mat, index_row, weight_row = item
        rows_in = normed[index_row]
        summed = jnp.zeros((slot_limit, D), jnp.float32)
        for quarter in range(N_REP):
            lower = quarter * block
            gate_act = jnp.dot(rows_in, gate_mat[:, lower:lower + block], preferred_element_type=jnp.float32)
            up_act = jnp.dot(rows_in, up_mat[:, lower:lower + block], preferred_element_type=jnp.float32)
            hidden = (jax.nn.silu(gate_act) * up_act).astype(jnp.bfloat16)
            piece = jnp.dot(hidden, down_mat[lower:lower + block, :], preferred_element_type=jnp.float32).astype(jnp.bfloat16)
            piece = lax.optimization_barrier(piece)
            summed = summed + piece.astype(jnp.float32)
        total = total.at[index_row].add(weight_row[:, None] * summed)
        return (total, None)
    expert_sum = lax.scan(expert_step, jnp.zeros((ROWS, D), jnp.float32), (w_gate, w_up, w_down, table, weight_table))[0]
    layer_out = (stream_f + expert_sum).astype(jnp.bfloat16)
    return (attn_latent, layer_out)
```

```python
import jax
import jax.numpy as jnp
from jax import lax
from jax.sharding import Mesh
from jax.sharding import PartitionSpec as P

TORUS = ("rep", "ep_0", "ep_1", "ep_2")
EP = ("ep_0", "ep_1", "ep_2")


score_scale = 192.0 ** (-0.5)
norm_eps = 1e-06
meta_lanes = 128

PHASE_AXES = ((2, 1, 0), (0, 2, 1))


def torus_pairs(phase, step):
    sizes = [lax.axis_size(a) for a in TORUS]
    pairs = []
    for src in range(sizes[0] * sizes[1] * sizes[2] * sizes[3]):
        rest, core = divmod(src, sizes[3])
        rest, z = divmod(rest, sizes[2])
        x, y = divmod(rest, sizes[1])
        at = [x, y, z]
        axis = PHASE_AXES[core][phase]
        at[axis] = (at[axis] + step) % sizes[axis]
        pairs.append((src, ((at[0] * sizes[1] + at[1]) * sizes[2] + at[2]) * sizes[3] + core))
    return pairs


def move(block, phase, step):
    return lax.ppermute(block, TORUS, torus_pairs(phase, step))


def swap(block):
    return lax.ppermute(block, "ep_2", [(0, 1), (1, 0)])


def widen(block):
    return block.astype(jnp.float32)


def narrow(block):
    return block.astype(jnp.bfloat16)


def spread_direct(block, phase):
    return [block, move(block, phase, 1), move(block, phase, -1), move(block, phase, 2)]


def fold_direct(own, behind, ahead, across, phase):
    got = [move(behind, phase, -1), move(ahead, phase, 1), move(across, phase, 2)]
    return widen(own) + widen(got[0]) + widen(got[1]) + widen(got[2])


def spread_ring(block, phase):
    half = block.shape[0] // 2
    behind = move(block, phase, 1)
    ahead = move(block, phase, -1)
    across_a = move(behind[:half], phase, 1)
    across_b = move(ahead[half:], phase, -1)
    return [block, behind, ahead, across_a, across_b]


def fold_ring(own, behind, ahead, across_a, across_b, phase):
    half = own.shape[0] // 2
    via_a = move(narrow(across_a), phase, -1)
    via_b = move(narrow(across_b), phase, 1)
    behind = jnp.concatenate([narrow(widen(behind[:half]) + widen(via_a)), narrow(behind[half:])])
    ahead = jnp.concatenate([narrow(ahead[:half]), narrow(widen(ahead[half:]) + widen(via_b))])
    got_a = move(behind, phase, -1)
    got_b = move(ahead, phase, 1)
    return widen(own) + widen(got_a) + widen(got_b)


def hidden_of(blocks, w_gate, w_up, first_expert):
    rows = jnp.concatenate(blocks)
    width = w_gate.shape[1]
    tokens = rows[:, :width]
    chosen = widen(rows[:, width : width + 8])
    weight = widen(rows[:, width + 8 : width + 16])
    parts = []
    for e in range(w_gate.shape[0]):
        share = jnp.sum(jnp.where(chosen == (first_expert + e), weight, 0.0), axis=1, keepdims=True)
        gate = jnp.dot(tokens, w_gate[e], preferred_element_type=jnp.float32)
        up = jnp.dot(tokens, w_up[e], preferred_element_type=jnp.float32)
        parts.append(narrow(jax.nn.silu(gate) * up * share))
    return jnp.concatenate(parts, axis=1)


def attention(q_latent, q_rope, cache_latent, cache_rope, cache_len):
    scores = (
        jnp.einsum("ihl,itl->iht", q_latent, cache_latent, preferred_element_type=jnp.float32)
        + jnp.einsum("ihr,itr->iht", q_rope, cache_rope, preferred_element_type=jnp.float32)
    ) * score_scale
    valid_mask = (
        jnp.arange(cache_latent.shape[1], dtype=jnp.int32)[None, None, :] < cache_len[:, None, None]
    )
    scores = jnp.where(valid_mask, scores, -1e30)
    top_score = jnp.max(scores, axis=-1, keepdims=True)
    exponent = jnp.where(valid_mask, jnp.exp(scores - top_score), 0.0)
    attn_weights = (exponent / jnp.sum(exponent, axis=-1, keepdims=True)).astype(jnp.bfloat16)
    return jnp.einsum(
        "iht,itl->ihl", attn_weights, cache_latent, preferred_element_type=jnp.float32
    ).astype(jnp.bfloat16)


def per_device(
    q_latent,
    q_rope,
    cache_latent,
    cache_rope,
    cache_len,
    stream,
    norm_gain,
    expert_ids,
    route_weights,
    w_gate,
    w_up,
    w_down,
):
    row_count, width = stream.shape
    local_count = w_gate.shape[0]
    first_expert = (lax.axis_index(EP) * local_count).astype(jnp.float32)
    stream_f = widen(stream)
    normed = narrow(
        stream_f
        * lax.rsqrt(jnp.mean(stream_f * stream_f, axis=-1, keepdims=True) + norm_eps)
        * norm_gain
    )
    meta = jnp.concatenate([expert_ids.astype(jnp.bfloat16), route_weights], axis=1)
    meta = jnp.pad(meta, ((0, 0), (0, meta_lanes - meta.shape[1])))
    payload = jnp.concatenate([normed, meta], axis=1)

    line = jnp.concatenate(spread_direct(payload, 0))
    plane = jnp.concatenate(spread_ring(line, 1))
    own, behind, ahead, across_a, across_b = spread_ring(plane, 2)
    own_2 = swap(own)
    behind_2 = swap(behind)
    ahead_2 = swap(ahead)
    across = jnp.concatenate([across_a, across_b])
    across_2 = swap(across)

    block = own.shape[0]
    down = w_down.reshape(-1, width)

    def outputs(hidden):
        return jnp.dot(hidden, down, preferred_element_type=jnp.float32)

    hid_own = hidden_of([own, own_2], w_gate, w_up, first_expert)
    hid_near = hidden_of([behind, ahead], w_gate, w_up, first_expert)
    hid_near_2 = hidden_of([behind_2, ahead_2], w_gate, w_up, first_expert)
    hid_far = hidden_of([across, across_2], w_gate, w_up, first_expert)

    far_got = swap(narrow(outputs(hid_far[block:])))
    far = outputs(hid_far[:block]) + widen(far_got)
    near_got = swap(narrow(outputs(hid_near_2)))
    near = outputs(hid_near) + widen(near_got)
    own_got = swap(narrow(outputs(hid_own[block:])))
    mine = outputs(hid_own[:block]) + widen(own_got)

    plane_sum = fold_ring(
        mine, near[:block], near[block:], far[: block // 2], far[block // 2 :], 2
    )
    quarter = block // 4
    plane_sum = narrow(plane_sum)
    line_sum = fold_ring(
        plane_sum[:quarter],
        plane_sum[quarter : 2 * quarter],
        plane_sum[2 * quarter : 3 * quarter],
        plane_sum[3 * quarter : 3 * quarter + quarter // 2],
        plane_sum[3 * quarter + quarter // 2 :],
        1,
    )
    line_sum = narrow(line_sum)
    expert_sum = fold_direct(
        line_sum[:row_count],
        line_sum[row_count : 2 * row_count],
        line_sum[2 * row_count : 3 * row_count],
        line_sum[3 * row_count :],
        0,
    )
    layer_out = narrow(stream_f + expert_sum)
    attn_latent = attention(q_latent, q_rope, cache_latent, cache_rope, cache_len)
    return (attn_latent, layer_out)


def solution(mesh):
    sizes = mesh.shape
    torus = Mesh(mesh.devices.reshape(sizes["rep"], 4, 4, 2), TORUS)
    return jax.shard_map(
        per_device,
        mesh=torus,
        in_specs=(
            P(TORUS, None, None),
            P(TORUS, None, None),
            P(TORUS, None, None),
            P(TORUS, None, None),
            P(TORUS),
            P(TORUS, None),
            P(),
            P(TORUS, None),
            P(TORUS, None),
            P(EP, None, "rep"),
            P(EP, None, "rep"),
            P(EP, "rep", None),
        ),
        out_specs=(P(TORUS, None, None), P(TORUS, None)),
        check_vma=False,
    )
```

```python
import jax
import jax.numpy as jnp
from jax import lax
from jax.experimental import pallas as pl
from jax.experimental.pallas import tpu as pltpu
from jax.sharding import Mesh
from jax.sharding import PartitionSpec as P


TORUS = ("rep", "ep_0", "ep_1", "ep_2")
EP = ("ep_0", "ep_1", "ep_2")


score_scale = 192.0 ** (-0.5)
norm_eps = 1e-06
meta_lanes = 128
vmem_share = 16 << 20

PHASE_AXES = ((2, 1, 0), (0, 2, 1))


def torus_pairs(phase, step):
    sizes = [lax.axis_size(a) for a in TORUS]
    pairs = []
    for src in range(sizes[0] * sizes[1] * sizes[2] * sizes[3]):
        rest, core = divmod(src, sizes[3])
        rest, z = divmod(rest, sizes[2])
        x, y = divmod(rest, sizes[1])
        at = [x, y, z]
        axis = PHASE_AXES[core][phase]
        at[axis] = (at[axis] + step) % sizes[axis]
        pairs.append((src, ((at[0] * sizes[1] + at[1]) * sizes[2] + at[2]) * sizes[3] + core))
    return pairs


def move(block, phase, step):
    return lax.ppermute(block, TORUS, torus_pairs(phase, step))


def swap(block):
    return lax.ppermute(block, "ep_2", [(0, 1), (1, 0)])


def after(values):
    return lax.optimization_barrier(values)


def widen(block):
    return block.astype(jnp.float32)


def narrow(block):
    return block.astype(jnp.bfloat16)


def spread_direct(block, phase):
    return [block, move(block, phase, 1), move(block, phase, -1), move(block, phase, 2)]


def fold_direct(own, behind, ahead, across, phase):
    got = [move(behind, phase, -1), move(ahead, phase, 1), move(across, phase, 2)]
    return widen(own) + widen(got[0]) + widen(got[1]) + widen(got[2])


def spread_ring(block, phase):
    half = block.shape[0] // 2
    behind = move(block, phase, 1)
    ahead = move(block, phase, -1)
    across_a = move(behind[:half], phase, 1)
    across_b = move(ahead[half:], phase, -1)
    return [block, behind, ahead, across_a, across_b]


def fold_ring(own, behind, ahead, across_a, across_b, phase):
    half = own.shape[0] // 2
    via_a = move(narrow(across_a), phase, -1)
    via_b = move(narrow(across_b), phase, 1)
    behind = jnp.concatenate([narrow(widen(behind[:half]) + widen(via_a)), narrow(behind[half:])])
    ahead = jnp.concatenate([narrow(ahead[:half]), narrow(widen(ahead[half:]) + widen(via_b))])
    got_a = move(behind, phase, -1)
    got_b = move(ahead, phase, 1)
    return widen(own) + widen(got_a) + widen(got_b)


def prepare(stream, norm_gain, expert_ids, route_weights):
    row_count, width = stream.shape

    def kernel(stream_ref, gain_ref, ids_ref, weights_ref, out_ref):
        rows = widen(stream_ref[...])
        scale = lax.rsqrt(jnp.mean(rows * rows, axis=-1, keepdims=True) + norm_eps)
        out_ref[:, :width] = narrow(rows * scale * gain_ref[...])
        ids = ids_ref[...]
        weights = widen(weights_ref[...])
        lane = lax.broadcasted_iota(jnp.int32, (row_count, meta_lanes), 1)
        table = jnp.zeros((row_count, meta_lanes), jnp.float32)
        for k in range(ids.shape[1]):
            table = jnp.where(lane == ids[:, k : k + 1], weights[:, k : k + 1], table)
        out_ref[:, width:] = narrow(table)

    return pl.pallas_call(
        kernel,
        out_shape=jax.ShapeDtypeStruct((row_count, width + meta_lanes), jnp.bfloat16),
        name="prepare",
    )(stream, norm_gain.reshape(1, -1), expert_ids, route_weights)


def resident(*arrays):
    count = len(arrays)

    def kernel(*refs):
        sources, targets, sems = refs[:count], refs[count : 2 * count], refs[2 * count]
        copies = [
            pltpu.make_async_copy(sources[i], targets[i], sems.at[i]) for i in range(count)
        ]
        for copy in copies:
            copy.start()
        for copy in copies:
            copy.wait()

    return pl.pallas_call(
        kernel,
        in_specs=[pl.BlockSpec(memory_space=pltpu.HBM)] * count,
        out_specs=[pl.BlockSpec(memory_space=pltpu.VMEM)] * count,
        out_shape=[pltpu.VMEM(a.shape, a.dtype) for a in arrays],
        scratch_shapes=[pltpu.SemaphoreType.DMA((count,))],
        compiler_params=pltpu.CompilerParams(vmem_limit_bytes=vmem_share),
        name="resident",
    )(*[pltpu.with_memory_space_constraint(a, pltpu.HBM) for a in arrays])


def hidden_of(blocks, w_gate, w_up, first_expert):
    local_count, width, units = w_gate.shape
    steps = 2
    tile = width // steps
    sizes = [b.shape[0] for b in blocks]
    total = sum(sizes)
    count = len(blocks)

    def kernel(first_ref, *refs):
        rows_refs, meta_refs = refs[:count], refs[count : 2 * count]
        gate_ref, up_ref, out_ref, acc_ref = refs[2 * count :]
        step = pl.program_id(0)

        @pl.when(step == 0)
        def _():
            acc_ref[...] = jnp.zeros_like(acc_ref)

        rows = jnp.concatenate([r[...] for r in rows_refs], axis=0)
        for e in range(local_count):
            gate = gate_ref[e, pl.ds(step * tile, tile), :]
            up = up_ref[e, pl.ds(step * tile, tile), :]
            acc_ref[2 * e] += jnp.dot(rows, gate, preferred_element_type=jnp.float32)
            acc_ref[2 * e + 1] += jnp.dot(rows, up, preferred_element_type=jnp.float32)

        @pl.when(step == steps - 1)
        def _():
            meta = widen(jnp.concatenate([r[...] for r in meta_refs], axis=0))
            lane = lax.broadcasted_iota(jnp.int32, meta.shape, 1)
            for e in range(local_count):
                mine = jnp.where(lane == first_ref[0] + e, meta, 0.0)
                share = jnp.sum(mine, axis=1, keepdims=True)
                act = jax.nn.silu(acc_ref[2 * e]) * acc_ref[2 * e + 1] * share
                out_ref[:, e * units : (e + 1) * units] = narrow(act)

    return pl.pallas_call(
        kernel,
        grid=(steps,),
        in_specs=[pl.BlockSpec(memory_space=pltpu.SMEM)]
        + [pl.BlockSpec((n, tile), lambda k: (0, k)) for n in sizes]
        + [pl.BlockSpec((n, meta_lanes), lambda k: (0, width // meta_lanes)) for n in sizes]
        + [pl.BlockSpec(memory_space=pltpu.VMEM)] * 2,
        out_specs=pl.BlockSpec((total, local_count * units), lambda k: (0, 0)),
        out_shape=jax.ShapeDtypeStruct((total, local_count * units), jnp.bfloat16),
        scratch_shapes=[pltpu.VMEM((2 * local_count, total, units), jnp.float32)],
        compiler_params=pltpu.CompilerParams(vmem_limit_bytes=vmem_share),
        cost_estimate=pl.CostEstimate(
            flops=4 * total * width * units * local_count,
            transcendentals=total * units * local_count,
            bytes_accessed=4 * width * units * local_count + 2 * total * width,
        ),
        name="hidden",
    )(first_expert, *blocks, *blocks, w_gate, w_up)


def outputs_of(hidden, block, sizes, down, got=None):
    width = down.shape[2]
    inner = hidden.shape[1]
    steps = 4
    tile = width // steps
    total = sum(sizes)

    def kernel(*refs):
        hidden_ref, down_ref = refs[:2]
        out_refs = refs[-len(sizes) :]
        here = pl.ds(pl.multiple_of(pl.program_id(0) * tile, 128), tile)
        hidden_rows = hidden_ref[...]
        units = inner // down_ref.shape[0]
        part = jnp.zeros((total, tile), jnp.float32)
        for e in range(down_ref.shape[0]):
            part = part + jnp.dot(
                hidden_rows[:, e * units : (e + 1) * units],
                down_ref[e, :, here],
                preferred_element_type=jnp.float32,
            )
        if got is not None:
            part = part + widen(refs[2][...])
        at = 0
        for n, out_ref in zip(sizes, out_refs):
            out_ref[...] = narrow(part[at : at + n])
            at += n

    specs = [
        pl.BlockSpec((total, inner), lambda n: (block, 0)),
        pl.BlockSpec(memory_space=pltpu.VMEM),
    ]
    operands = [hidden, down]
    if got is not None:
        specs.append(pl.BlockSpec((total, tile), lambda n: (0, n)))
        operands.append(got)
    return pl.pallas_call(
        kernel,
        grid=(steps,),
        in_specs=specs,
        out_specs=[pl.BlockSpec((n, tile), lambda n: (0, n)) for n in sizes],
        out_shape=[jax.ShapeDtypeStruct((n, width), jnp.bfloat16) for n in sizes],
        compiler_params=pltpu.CompilerParams(vmem_limit_bytes=vmem_share),
        cost_estimate=pl.CostEstimate(
            flops=2 * total * inner * width,
            transcendentals=0,
            bytes_accessed=2 * inner * width + 4 * total * width,
        ),
        name="outputs",
    )(*operands)


def attention(q_latent, q_rope, cache_latent, cache_rope, cache_len):
    scores = (
        jnp.einsum("ihl,itl->iht", q_latent, cache_latent, preferred_element_type=jnp.float32)
        + jnp.einsum("ihr,itr->iht", q_rope, cache_rope, preferred_element_type=jnp.float32)
    ) * score_scale
    valid_mask = (
        jnp.arange(cache_latent.shape[1], dtype=jnp.int32)[None, None, :] < cache_len[:, None, None]
    )
    scores = jnp.where(valid_mask, scores, -1e30)
    top_score = jnp.max(scores, axis=-1, keepdims=True)
    exponent = jnp.where(valid_mask, jnp.exp(scores - top_score), 0.0)
    attn_weights = (exponent / jnp.sum(exponent, axis=-1, keepdims=True)).astype(jnp.bfloat16)
    return jnp.einsum(
        "iht,itl->ihl", attn_weights, cache_latent, preferred_element_type=jnp.float32
    ).astype(jnp.bfloat16)


def layer(
    q_latent,
    q_rope,
    cache_latent,
    cache_rope,
    cache_len,
    stream,
    norm_gain,
    expert_ids,
    route_weights,
    w_gate,
    w_up,
    w_down,
):
    row_count, _ = stream.shape
    local_count = w_gate.shape[0]
    first_expert = (lax.axis_index(EP) * local_count).astype(jnp.int32).reshape(1)
    stream_f = widen(stream)
    payload = prepare(stream, norm_gain, expert_ids, route_weights)

    line = jnp.concatenate(spread_direct(payload, 0))
    plane = jnp.concatenate(spread_ring(line, 1))
    block = plane.shape[0]
    half = block // 2
    behind = move(plane, 2, 1)
    ahead = move(plane, 2, -1)
    plane_2 = swap(plane)
    w_gate, w_up, down = resident(w_gate, w_up, w_down)
    hid_own = hidden_of([plane, plane_2], w_gate, w_up, first_expert)
    (own_2,) = outputs_of(hid_own, 1, [block], down)
    own_got = swap(own_2)
    (mine,) = outputs_of(hid_own, 0, [block], down, own_got)

    behind, ahead, mine = after((behind, ahead, mine))
    across_a = move(behind[:half], 2, 1)
    across_b = move(ahead[half:], 2, -1)
    behind_2 = swap(behind)
    ahead_2 = swap(ahead)
    hid_near = hidden_of([behind, ahead], w_gate, w_up, first_expert)
    behind_2, ahead_2, hid_near = after((behind_2, ahead_2, hid_near))
    hid_near_2 = hidden_of([behind_2, ahead_2], w_gate, w_up, first_expert)

    across_a, across_b, hid_near_2 = after((across_a, across_b, hid_near_2))
    across_a2 = swap(across_a)
    across_b2 = swap(across_b)
    (near_2,) = outputs_of(hid_near_2, 0, [2 * block], down)
    across_a2, across_b2, near_2 = after((across_a2, across_b2, near_2))
    near_got = swap(near_2)
    hid_far = hidden_of([across_a, across_b, across_a2, across_b2], w_gate, w_up, first_expert)
    (far_2,) = outputs_of(hid_far, 1, [block], down)
    hid_near, far_2 = after((hid_near, far_2))
    far_got = swap(far_2)
    near_a, near_b = outputs_of(hid_near, 0, [block, block], down, near_got)
    hid_far, near_a, near_b = after((hid_far, near_a, near_b))
    far_a, far_b = outputs_of(hid_far, 0, [half, half], down, far_got)

    plane_sum = fold_ring(mine, near_a, near_b, far_a, far_b, 2)
    quarter = block // 4
    plane_sum = narrow(plane_sum)
    line_sum = fold_ring(
        plane_sum[:quarter],
        plane_sum[quarter : 2 * quarter],
        plane_sum[2 * quarter : 3 * quarter],
        plane_sum[3 * quarter : 3 * quarter + quarter // 2],
        plane_sum[3 * quarter + quarter // 2 :],
        1,
    )
    line_sum = narrow(line_sum)
    expert_sum = fold_direct(
        line_sum[:row_count],
        line_sum[row_count : 2 * row_count],
        line_sum[2 * row_count : 3 * row_count],
        line_sum[3 * row_count :],
        0,
    )
    layer_out = narrow(stream_f + expert_sum)
    attn_latent = attention(q_latent, q_rope, cache_latent, cache_rope, cache_len)
    return (attn_latent, layer_out)


def solution(mesh):
    sizes = mesh.shape
    torus = Mesh(mesh.devices.reshape(sizes["rep"], 4, 4, 2), TORUS)
    return jax.shard_map(
        layer,
        mesh=torus,
        in_specs=(
            P(TORUS, None, None),
            P(TORUS, None, None),
            P(TORUS, None, None),
            P(TORUS, None, None),
            P(TORUS),
            P(TORUS, None),
            P(),
            P(TORUS, None),
            P(TORUS, None),
            P(EP, None, "rep"),
            P(EP, None, "rep"),
            P(EP, "rep", None),
        ),
        out_specs=(P(TORUS, None, None), P(TORUS, None)),
        check_vma=False,
    )
```

```python
import jax
import jax.numpy as jnp
from jax import lax
from jax.experimental import pallas as pl
from jax.experimental.pallas import tpu as pltpu
from jax.sharding import Mesh
from jax.sharding import PartitionSpec as P


TORUS = ("rep", "ep_0", "ep_1", "ep_2")
EP = ("ep_0", "ep_1", "ep_2")


score_scale = 192.0 ** (-0.5)
norm_eps = 1e-06
meta_lanes = 128
vmem_share = 8 << 20

PHASE_AXES = ((2, 1, 0), (0, 2, 1))


def torus_pairs(phase, step):
    sizes = [lax.axis_size(a) for a in TORUS]
    pairs = []
    for src in range(sizes[0] * sizes[1] * sizes[2] * sizes[3]):
        rest, core = divmod(src, sizes[3])
        rest, z = divmod(rest, sizes[2])
        x, y = divmod(rest, sizes[1])
        at = [x, y, z]
        axis = PHASE_AXES[core][phase]
        at[axis] = (at[axis] + step) % sizes[axis]
        pairs.append((src, ((at[0] * sizes[1] + at[1]) * sizes[2] + at[2]) * sizes[3] + core))
    return pairs


def move(block, phase, step):
    return lax.ppermute(block, TORUS, torus_pairs(phase, step))


def swap(block):
    return lax.ppermute(block, "ep_2", [(0, 1), (1, 0)])


def after(values):
    return lax.optimization_barrier(values)


def widen(block):
    return block.astype(jnp.float32)


def narrow(block):
    return block.astype(jnp.bfloat16)


def spread_direct(block, phase):
    return [block, move(block, phase, 1), move(block, phase, -1), move(block, phase, 2)]


def fold_direct(own, behind, ahead, across, phase):
    got = [move(behind, phase, -1), move(ahead, phase, 1), move(across, phase, 2)]
    return widen(own) + widen(got[0]) + widen(got[1]) + widen(got[2])


def pack(blocks):
    count = len(blocks)
    sizes = [b.shape[0] for b in blocks]

    def kernel(*refs):
        out_ref = refs[-1]
        at = 0
        for ref, n in zip(refs[:count], sizes):
            out_ref[at : at + n] = ref[...]
            at += n

    return pl.pallas_call(
        kernel,
        in_specs=[pl.BlockSpec(memory_space=pltpu.VMEM)] * count,
        out_shape=jax.ShapeDtypeStruct((sum(sizes), blocks[0].shape[1]), blocks[0].dtype),
        compiler_params=pltpu.CompilerParams(vmem_limit_bytes=vmem_share),
        name="pack",
    )(*blocks)


def merge(block, via, at, via_at, count):
    rows = block.shape[0]

    def kernel(block_ref, via_ref, out_ref):
        if at:
            out_ref[:at] = block_ref[:at]
        added = widen(block_ref[at : at + count]) + widen(via_ref[via_at : via_at + count])
        out_ref[at : at + count] = narrow(added)
        if at + count < rows:
            out_ref[at + count :] = block_ref[at + count :]

    return pl.pallas_call(
        kernel,
        out_shape=jax.ShapeDtypeStruct(block.shape, block.dtype),
        compiler_params=pltpu.CompilerParams(vmem_limit_bytes=vmem_share),
        name="merge",
    )(block, via)


def prepare(stream, norm_gain, expert_ids, route_weights):
    row_count, width = stream.shape

    def kernel(stream_ref, gain_ref, ids_ref, weights_ref, out_ref):
        rows = widen(stream_ref[...])
        scale = lax.rsqrt(jnp.mean(rows * rows, axis=-1, keepdims=True) + norm_eps)
        out_ref[:, :width] = narrow(rows * scale * gain_ref[...])
        ids = ids_ref[...]
        weights = widen(weights_ref[...])
        lane = lax.broadcasted_iota(jnp.int32, (row_count, meta_lanes), 1)
        table = jnp.zeros((row_count, meta_lanes), jnp.float32)
        for k in range(ids.shape[1]):
            table = jnp.where(lane == ids[:, k : k + 1], weights[:, k : k + 1], table)
        out_ref[:, width:] = narrow(table)

    return pl.pallas_call(
        kernel,
        out_shape=jax.ShapeDtypeStruct((row_count, width + meta_lanes), jnp.bfloat16),
        name="prepare",
    )(stream, norm_gain.reshape(1, -1), expert_ids, route_weights)


def finish(acc_ref, meta, first, out_ref, local_count, units):
    lane = lax.broadcasted_iota(jnp.int32, meta.shape, 1)
    for e in range(local_count):
        mine = jnp.where(lane == first + e, widen(meta), 0.0)
        share = jnp.sum(mine, axis=1, keepdims=True)
        act = jax.nn.silu(acc_ref[2 * e]) * acc_ref[2 * e + 1] * share
        out_ref[:, e * units : (e + 1) * units] = narrow(act)


def first_hidden(blocks, w_gate, w_up, w_down, first_expert):
    local_count, width, units = w_gate.shape
    steps = 7
    tile = width // steps
    total = sum(b.shape[0] for b in blocks)
    count = len(blocks)

    def kernel(first_ref, *refs):
        rows_refs = refs[:count]
        sources = refs[count : count + 3]
        out_ref, gate_ref, up_ref, down_ref, acc_ref, sems, down_sem = refs[count + 3 :]

        def piece(k, which):
            here = pl.ds(k * tile, tile)
            target = (gate_ref, up_ref)[which]
            return pltpu.make_async_copy(
                sources[which].at[:, here, :], target.at[:, here, :], sems.at[k, which]
            )

        for k in range(steps):
            piece(k, 0).start()
            piece(k, 1).start()
        last = pltpu.make_async_copy(sources[2], down_ref, down_sem)
        last.start()
        for k in range(steps):
            here = slice(k * tile, (k + 1) * tile)
            rows = jnp.concatenate([r[:, here] for r in rows_refs], axis=0)
            for which, ref in enumerate((gate_ref, up_ref)):
                piece(k, which).wait()
                for e in range(local_count):
                    part = jnp.dot(rows, ref[e, here, :], preferred_element_type=jnp.float32)
                    if k:
                        part = part + acc_ref[2 * e + which]
                    acc_ref[2 * e + which] = part
        meta = jnp.concatenate([r[:, width:] for r in rows_refs], axis=0)
        finish(acc_ref, meta, first_ref[0], out_ref, local_count, units)
        last.wait()

    weights = (w_gate, w_up, w_down)
    return pl.pallas_call(
        kernel,
        in_specs=[pl.BlockSpec(memory_space=pltpu.SMEM)]
        + [pl.BlockSpec(memory_space=pltpu.VMEM)] * count
        + [pl.BlockSpec(memory_space=pltpu.HBM)] * 3,
        out_specs=[pl.BlockSpec(memory_space=pltpu.VMEM)] * 4,
        out_shape=[jax.ShapeDtypeStruct((total, local_count * units), jnp.bfloat16)]
        + [pltpu.VMEM(w.shape, w.dtype) for w in weights],
        scratch_shapes=[
            pltpu.VMEM((2 * local_count, total, units), jnp.float32),
            pltpu.SemaphoreType.DMA((steps, 2)),
            pltpu.SemaphoreType.DMA,
        ],
        compiler_params=pltpu.CompilerParams(vmem_limit_bytes=vmem_share + (4 << 20)),
        cost_estimate=pl.CostEstimate(
            flops=4 * total * width * units * local_count,
            transcendentals=total * units * local_count,
            bytes_accessed=6 * width * units * local_count,
        ),
        name="first_hidden",
    )(
        first_expert,
        *blocks,
        *[pltpu.with_memory_space_constraint(w, pltpu.HBM) for w in weights],
    )


def hidden_of(blocks, w_gate, w_up, first_expert):
    local_count, width, units = w_gate.shape
    steps = 2
    tile = width // steps
    sizes = [b.shape[0] for b in blocks]
    total = sum(sizes)
    count = len(blocks)

    def kernel(first_ref, *refs):
        rows_refs, meta_refs = refs[:count], refs[count : 2 * count]
        gate_ref, up_ref, out_ref, acc_ref = refs[2 * count :]
        step = pl.program_id(0)

        @pl.when(step == 0)
        def _():
            acc_ref[...] = jnp.zeros_like(acc_ref)

        rows = jnp.concatenate([r[...] for r in rows_refs], axis=0)
        for e in range(local_count):
            gate = gate_ref[e, pl.ds(step * tile, tile), :]
            up = up_ref[e, pl.ds(step * tile, tile), :]
            acc_ref[2 * e] += jnp.dot(rows, gate, preferred_element_type=jnp.float32)
            acc_ref[2 * e + 1] += jnp.dot(rows, up, preferred_element_type=jnp.float32)

        @pl.when(step == steps - 1)
        def _():
            meta = jnp.concatenate([r[...] for r in meta_refs], axis=0)
            finish(acc_ref, meta, first_ref[0], out_ref, local_count, units)

    return pl.pallas_call(
        kernel,
        grid=(steps,),
        in_specs=[pl.BlockSpec(memory_space=pltpu.SMEM)]
        + [pl.BlockSpec((n, tile), lambda k: (0, k)) for n in sizes]
        + [pl.BlockSpec((n, meta_lanes), lambda k: (0, width // meta_lanes)) for n in sizes]
        + [pl.BlockSpec(memory_space=pltpu.VMEM)] * 2,
        out_specs=pl.BlockSpec((total, local_count * units), lambda k: (0, 0)),
        out_shape=jax.ShapeDtypeStruct((total, local_count * units), jnp.bfloat16),
        scratch_shapes=[pltpu.VMEM((2 * local_count, total, units), jnp.float32)],
        compiler_params=pltpu.CompilerParams(vmem_limit_bytes=vmem_share),
        cost_estimate=pl.CostEstimate(
            flops=4 * total * width * units * local_count,
            transcendentals=total * units * local_count,
            bytes_accessed=4 * width * units * local_count + 2 * total * width,
        ),
        name="hidden",
    )(first_expert, *blocks, *blocks, w_gate, w_up)


def outputs_of(hidden, block, sizes, down, got=None):
    width = down.shape[2]
    inner = hidden.shape[1]
    steps = 4
    tile = width // steps
    total = sum(sizes)

    def kernel(*refs):
        hidden_ref, down_ref = refs[:2]
        out_refs = refs[-len(sizes) :]
        here = pl.ds(pl.multiple_of(pl.program_id(0) * tile, 128), tile)
        hidden_rows = hidden_ref[...]
        units = inner // down_ref.shape[0]
        part = jnp.zeros((total, tile), jnp.float32)
        for e in range(down_ref.shape[0]):
            part = part + jnp.dot(
                hidden_rows[:, e * units : (e + 1) * units],
                down_ref[e, :, here],
                preferred_element_type=jnp.float32,
            )
        if got is not None:
            part = part + widen(refs[2][...])
        at = 0
        for n, out_ref in zip(sizes, out_refs):
            out_ref[...] = narrow(part[at : at + n])
            at += n

    specs = [
        pl.BlockSpec((total, inner), lambda n: (block, 0)),
        pl.BlockSpec(memory_space=pltpu.VMEM),
    ]
    operands = [hidden, down]
    if got is not None:
        specs.append(pl.BlockSpec((total, tile), lambda n: (0, n)))
        operands.append(got)
    return pl.pallas_call(
        kernel,
        grid=(steps,),
        in_specs=specs,
        out_specs=[pl.BlockSpec((n, tile), lambda n: (0, n)) for n in sizes],
        out_shape=[jax.ShapeDtypeStruct((n, width), jnp.bfloat16) for n in sizes],
        compiler_params=pltpu.CompilerParams(vmem_limit_bytes=vmem_share),
        cost_estimate=pl.CostEstimate(
            flops=2 * total * inner * width,
            transcendentals=0,
            bytes_accessed=2 * inner * width + 4 * total * width,
        ),
        name="outputs",
    )(*operands)


def attention(q_latent, q_rope, cache_latent, cache_rope, cache_len):
    scores = (
        jnp.einsum("ihl,itl->iht", q_latent, cache_latent, preferred_element_type=jnp.float32)
        + jnp.einsum("ihr,itr->iht", q_rope, cache_rope, preferred_element_type=jnp.float32)
    ) * score_scale
    valid_mask = (
        jnp.arange(cache_latent.shape[1], dtype=jnp.int32)[None, None, :] < cache_len[:, None, None]
    )
    scores = jnp.where(valid_mask, scores, -1e30)
    top_score = jnp.max(scores, axis=-1, keepdims=True)
    exponent = jnp.where(valid_mask, jnp.exp(scores - top_score), 0.0)
    attn_weights = (exponent / jnp.sum(exponent, axis=-1, keepdims=True)).astype(jnp.bfloat16)
    return jnp.einsum(
        "iht,itl->ihl", attn_weights, cache_latent, preferred_element_type=jnp.float32
    ).astype(jnp.bfloat16)


def layer(
    q_latent,
    q_rope,
    cache_latent,
    cache_rope,
    cache_len,
    stream,
    norm_gain,
    expert_ids,
    route_weights,
    w_gate,
    w_up,
    w_down,
):
    row_count, _ = stream.shape
    local_count = w_gate.shape[0]
    first_expert = (lax.axis_index(EP) * local_count).astype(jnp.int32).reshape(1)
    stream_f = widen(stream)
    payload = prepare(stream, norm_gain, expert_ids, route_weights)

    line = jnp.concatenate(spread_direct(payload, 0))
    size = line.shape[0]
    half = size // 2
    near_rows = 3 * size
    near_half = near_rows // 2
    block = 4 * size

    line_behind = move(line, 1, 1)
    line_ahead = move(line, 1, -1)
    line_far_a = move(line_behind[:half], 1, 1)
    line_far_b = move(line_ahead[half:], 1, -1)
    own_a = pack([line, line_behind, line_ahead])
    behind_a = move(own_a, 2, 1)
    ahead_a = move(own_a, 2, -1)
    own_b = pack([line_far_a, line_far_b])
    behind_b = move(own_b, 2, 1)
    ahead_b = move(own_b, 2, -1)
    own_a2 = swap(own_a)
    own_b2 = swap(own_b)
    hid_own, w_gate, w_up, down = first_hidden(
        [own_a, own_b, own_a2, own_b2], w_gate, w_up, w_down, first_expert
    )
    far_wide_a = move(behind_a[:near_half], 2, 1)
    far_wide_b = move(ahead_a[near_half:], 2, -1)
    behind_a2 = swap(behind_a)
    ahead_a2 = swap(ahead_a)
    far_slim_a = move(behind_b[:half], 2, 1)
    far_slim_b = move(ahead_b[half:], 2, -1)
    behind_b2 = swap(behind_b)
    ahead_b2 = swap(ahead_b)
    hid_near = hidden_of([behind_a, behind_b, ahead_a, ahead_b], w_gate, w_up, first_expert)
    behind_a2, hid_near = after((behind_a2, hid_near))
    hid_near_2 = hidden_of([behind_a2, behind_b2, ahead_a2, ahead_b2], w_gate, w_up, first_expert)
    far = [far_wide_a, far_slim_a, far_wide_b, far_slim_b]
    far_2 = [swap(f) for f in far]
    (near_2,) = outputs_of(hid_near_2, 0, [2 * block], down)
    *far_2, near_2 = after((*far_2, near_2))
    near_got = swap(near_2)
    hid_far = hidden_of(far + far_2, w_gate, w_up, first_expert)
    (far_part,) = outputs_of(hid_far, 1, [block], down)
    hid_near, far_part = after((hid_near, far_part))
    far_got = swap(far_part)
    near = outputs_of(hid_near, 0, [near_rows, size, near_rows, size], down, near_got)
    hid_far, *near = after((hid_far, *near))
    far_a, far_b = outputs_of(hid_far, 0, [block // 2, block // 2], down, far_got)

    via_a = move(far_a, 2, -1)
    via_b = move(far_b, 2, 1)
    (own_2,) = outputs_of(hid_own, 1, [block], down)
    own_got = swap(own_2)
    mine_a, mine_b = outputs_of(hid_own, 0, [near_rows, size], down, own_got)
    behind_a, behind_b, ahead_a, ahead_b = near
    slim_got_a = move(merge(behind_b, via_a, 0, near_half, half), 2, -1)
    slim_got_b = move(merge(ahead_b, via_b, half, near_half, half), 2, 1)
    wide_got_a = move(merge(behind_a, via_a, 0, 0, near_half), 2, -1)
    wide_got_b = move(merge(ahead_a, via_b, near_half, 0, near_half), 2, 1)
    slim = narrow(widen(mine_b) + widen(slim_got_a) + widen(slim_got_b))
    line_via_a = move(slim[:half], 1, -1)
    line_via_b = move(slim[half:], 1, 1)
    wide = narrow(widen(mine_a) + widen(wide_got_a) + widen(wide_got_b))
    line_got_a = move(merge(wide[size : 2 * size], line_via_a, 0, 0, half), 1, -1)
    line_got_b = move(merge(wide[2 * size :], line_via_b, half, 0, half), 1, 1)
    line_sum = narrow(widen(wide[:size]) + widen(line_got_a) + widen(line_got_b))
    expert_sum = fold_direct(
        line_sum[:row_count],
        line_sum[row_count : 2 * row_count],
        line_sum[2 * row_count : 3 * row_count],
        line_sum[3 * row_count :],
        0,
    )
    layer_out = narrow(stream_f + expert_sum)
    attn_latent = attention(q_latent, q_rope, cache_latent, cache_rope, cache_len)
    return (attn_latent, layer_out)


def solution(mesh):
    sizes = mesh.shape
    torus = Mesh(mesh.devices.reshape(sizes["rep"], 4, 4, 2), TORUS)
    return jax.shard_map(
        layer,
        mesh=torus,
        in_specs=(
            P(TORUS, None, None),
            P(TORUS, None, None),
            P(TORUS, None, None),
            P(TORUS, None, None),
            P(TORUS),
            P(TORUS, None),
            P(),
            P(TORUS, None),
            P(TORUS, None),
            P(EP, None, "rep"),
            P(EP, None, "rep"),
            P(EP, "rep", None),
        ),
        out_specs=(P(TORUS, None, None), P(TORUS, None)),
        check_vma=False,
    )
```

```python
import jax
import jax.numpy as jnp
from jax import lax
from jax.experimental import pallas as pl
from jax.experimental.pallas import tpu as pltpu
from jax.sharding import Mesh
from jax.sharding import PartitionSpec as P


TORUS = ("rep", "ep_0", "ep_1", "ep_2")
EP = ("ep_0", "ep_1", "ep_2")


score_scale = 192.0 ** (-0.5)
norm_eps = 1e-06
meta_lanes = 128
vmem_share = 8 << 20

PHASE_AXES = ((2, 1, 0), (0, 2, 1))


def torus_pairs(phase, step):
    sizes = [lax.axis_size(a) for a in TORUS]
    pairs = []
    for src in range(sizes[0] * sizes[1] * sizes[2] * sizes[3]):
        rest, core = divmod(src, sizes[3])
        rest, z = divmod(rest, sizes[2])
        x, y = divmod(rest, sizes[1])
        at = [x, y, z]
        axis = PHASE_AXES[core][phase]
        at[axis] = (at[axis] + step) % sizes[axis]
        pairs.append((src, ((at[0] * sizes[1] + at[1]) * sizes[2] + at[2]) * sizes[3] + core))
    return pairs


def move(block, phase, step):
    return lax.ppermute(block, TORUS, torus_pairs(phase, step))


def swap(block):
    return lax.ppermute(block, "ep_2", [(0, 1), (1, 0)])


def after(values):
    return lax.optimization_barrier(values)


def widen(block):
    return block.astype(jnp.float32)


def narrow(block):
    return block.astype(jnp.bfloat16)


def spread_direct(block, phase):
    return [block, move(block, phase, 1), move(block, phase, -1), move(block, phase, 2)]


def fold_direct(own, behind, ahead, across, phase):
    got = [move(behind, phase, -1), move(ahead, phase, 1), move(across, phase, 2)]
    return widen(own) + widen(got[0]) + widen(got[1]) + widen(got[2])


def pack(blocks):
    count = len(blocks)
    sizes = [b.shape[0] for b in blocks]

    def kernel(*refs):
        out_ref = refs[-1]
        at = 0
        for ref, n in zip(refs[:count], sizes):
            out_ref[at : at + n] = ref[...]
            at += n

    return pl.pallas_call(
        kernel,
        in_specs=[pl.BlockSpec(memory_space=pltpu.VMEM)] * count,
        out_shape=jax.ShapeDtypeStruct((sum(sizes), blocks[0].shape[1]), blocks[0].dtype),
        compiler_params=pltpu.CompilerParams(vmem_limit_bytes=vmem_share),
        name="pack",
    )(*blocks)


def merge(block, via, at, via_at, count):
    rows = block.shape[0]

    def kernel(block_ref, via_ref, out_ref):
        if at:
            out_ref[:at] = block_ref[:at]
        added = widen(block_ref[at : at + count]) + widen(via_ref[via_at : via_at + count])
        out_ref[at : at + count] = narrow(added)
        if at + count < rows:
            out_ref[at + count :] = block_ref[at + count :]

    return pl.pallas_call(
        kernel,
        out_shape=jax.ShapeDtypeStruct(block.shape, block.dtype),
        compiler_params=pltpu.CompilerParams(vmem_limit_bytes=vmem_share),
        name="merge",
    )(block, via)


def settle(upper, lower, via_a, via_b):
    half, width = via_a.shape
    size = 2 * half

    def kernel(*refs):
        top = sum(widen(r[...]) for r in refs[:3])
        bottom = sum(widen(r[...]) for r in refs[3:6])
        first_ref, second_ref, third_ref = refs[8:]
        first_ref[...] = narrow(top[:size])
        second_ref[:half] = narrow(top[size:] + widen(refs[6][...]))
        second_ref[half:] = narrow(bottom[:half])
        third_ref[:half] = narrow(bottom[half:size])
        third_ref[half:] = narrow(bottom[size:] + widen(refs[7][...]))

    return pl.pallas_call(
        kernel,
        out_shape=[jax.ShapeDtypeStruct((size, width), via_a.dtype)] * 3,
        compiler_params=pltpu.CompilerParams(vmem_limit_bytes=vmem_share + (8 << 20)),
        name="settle",
    )(*upper, *lower, via_a, via_b)


def prepare(stream, norm_gain, expert_ids, route_weights):
    row_count, width = stream.shape

    def kernel(stream_ref, gain_ref, ids_ref, weights_ref, out_ref):
        rows = widen(stream_ref[...])
        scale = lax.rsqrt(jnp.mean(rows * rows, axis=-1, keepdims=True) + norm_eps)
        out_ref[:, :width] = narrow(rows * scale * gain_ref[...])
        ids = ids_ref[...]
        weights = widen(weights_ref[...])
        lane = lax.broadcasted_iota(jnp.int32, (row_count, meta_lanes), 1)
        table = jnp.zeros((row_count, meta_lanes), jnp.float32)
        for k in range(ids.shape[1]):
            table = jnp.where(lane == ids[:, k : k + 1], weights[:, k : k + 1], table)
        out_ref[:, width:] = narrow(table)

    return pl.pallas_call(
        kernel,
        out_shape=jax.ShapeDtypeStruct((row_count, width + meta_lanes), jnp.bfloat16),
        name="prepare",
    )(stream, norm_gain.reshape(1, -1), expert_ids, route_weights)


def finish(acc_ref, meta, first, out_ref, local_count, units):
    lane = lax.broadcasted_iota(jnp.int32, meta.shape, 1)
    for e in range(local_count):
        mine = jnp.where(lane == first + e, widen(meta), 0.0)
        share = jnp.sum(mine, axis=1, keepdims=True)
        act = jax.nn.silu(acc_ref[2 * e]) * acc_ref[2 * e + 1] * share
        out_ref[:, e * units : (e + 1) * units] = narrow(act)


def first_hidden(blocks, w_gate, w_up, w_down, first_expert):
    local_count, width, units = w_gate.shape
    steps = 7
    tile = width // steps
    total = sum(b.shape[0] for b in blocks)
    count = len(blocks)

    def kernel(first_ref, *refs):
        rows_refs = refs[:count]
        sources = refs[count : count + 3]
        out_ref, gate_ref, up_ref, down_ref, acc_ref, sems, down_sem = refs[count + 3 :]

        def piece(k, which):
            here = pl.ds(k * tile, tile)
            target = (gate_ref, up_ref)[which]
            return pltpu.make_async_copy(
                sources[which].at[:, here, :], target.at[:, here, :], sems.at[k, which]
            )

        for k in range(steps):
            piece(k, 0).start()
            piece(k, 1).start()
        last = pltpu.make_async_copy(sources[2], down_ref, down_sem)
        last.start()
        for k in range(steps):
            here = slice(k * tile, (k + 1) * tile)
            rows = jnp.concatenate([r[:, here] for r in rows_refs], axis=0)
            for which, ref in enumerate((gate_ref, up_ref)):
                piece(k, which).wait()
                for e in range(local_count):
                    part = jnp.dot(rows, ref[e, here, :], preferred_element_type=jnp.float32)
                    if k:
                        part = part + acc_ref[2 * e + which]
                    acc_ref[2 * e + which] = part
        meta = jnp.concatenate([r[:, width:] for r in rows_refs], axis=0)
        finish(acc_ref, meta, first_ref[0], out_ref, local_count, units)
        last.wait()

    weights = (w_gate, w_up, w_down)
    return pl.pallas_call(
        kernel,
        in_specs=[pl.BlockSpec(memory_space=pltpu.SMEM)]
        + [pl.BlockSpec(memory_space=pltpu.VMEM)] * count
        + [pl.BlockSpec(memory_space=pltpu.HBM)] * 3,
        out_specs=[pl.BlockSpec(memory_space=pltpu.VMEM)] * 4,
        out_shape=[jax.ShapeDtypeStruct((total, local_count * units), jnp.bfloat16)]
        + [pltpu.VMEM(w.shape, w.dtype) for w in weights],
        scratch_shapes=[
            pltpu.VMEM((2 * local_count, total, units), jnp.float32),
            pltpu.SemaphoreType.DMA((steps, 2)),
            pltpu.SemaphoreType.DMA,
        ],
        compiler_params=pltpu.CompilerParams(vmem_limit_bytes=vmem_share + (4 << 20)),
        cost_estimate=pl.CostEstimate(
            flops=4 * total * width * units * local_count,
            transcendentals=total * units * local_count,
            bytes_accessed=6 * width * units * local_count,
        ),
        name="first_hidden",
    )(
        first_expert,
        *blocks,
        *[pltpu.with_memory_space_constraint(w, pltpu.HBM) for w in weights],
    )


def hidden_of(blocks, w_gate, w_up, first_expert):
    local_count, width, units = w_gate.shape
    steps = 2
    tile = width // steps
    sizes = [b.shape[0] for b in blocks]
    total = sum(sizes)
    count = len(blocks)

    def kernel(first_ref, *refs):
        rows_refs, meta_refs = refs[:count], refs[count : 2 * count]
        gate_ref, up_ref, out_ref, acc_ref = refs[2 * count :]
        step = pl.program_id(0)

        @pl.when(step == 0)
        def _():
            acc_ref[...] = jnp.zeros_like(acc_ref)

        rows = jnp.concatenate([r[...] for r in rows_refs], axis=0)
        for e in range(local_count):
            gate = gate_ref[e, pl.ds(step * tile, tile), :]
            up = up_ref[e, pl.ds(step * tile, tile), :]
            acc_ref[2 * e] += jnp.dot(rows, gate, preferred_element_type=jnp.float32)
            acc_ref[2 * e + 1] += jnp.dot(rows, up, preferred_element_type=jnp.float32)

        @pl.when(step == steps - 1)
        def _():
            meta = jnp.concatenate([r[...] for r in meta_refs], axis=0)
            finish(acc_ref, meta, first_ref[0], out_ref, local_count, units)

    return pl.pallas_call(
        kernel,
        grid=(steps,),
        in_specs=[pl.BlockSpec(memory_space=pltpu.SMEM)]
        + [pl.BlockSpec((n, tile), lambda k: (0, k)) for n in sizes]
        + [pl.BlockSpec((n, meta_lanes), lambda k: (0, width // meta_lanes)) for n in sizes]
        + [pl.BlockSpec(memory_space=pltpu.VMEM)] * 2,
        out_specs=pl.BlockSpec((total, local_count * units), lambda k: (0, 0)),
        out_shape=jax.ShapeDtypeStruct((total, local_count * units), jnp.bfloat16),
        scratch_shapes=[pltpu.VMEM((2 * local_count, total, units), jnp.float32)],
        compiler_params=pltpu.CompilerParams(vmem_limit_bytes=vmem_share),
        cost_estimate=pl.CostEstimate(
            flops=4 * total * width * units * local_count,
            transcendentals=total * units * local_count,
            bytes_accessed=4 * width * units * local_count + 2 * total * width,
        ),
        name="hidden",
    )(first_expert, *blocks, *blocks, w_gate, w_up)


def outputs_of(hidden, block, sizes, down, got=None):
    width = down.shape[2]
    inner = hidden.shape[1]
    steps = 4
    tile = width // steps
    total = sum(sizes)

    def kernel(*refs):
        hidden_ref, down_ref = refs[:2]
        out_refs = refs[-len(sizes) :]
        here = pl.ds(pl.multiple_of(pl.program_id(0) * tile, 128), tile)
        hidden_rows = hidden_ref[...]
        units = inner // down_ref.shape[0]
        part = jnp.zeros((total, tile), jnp.float32)
        for e in range(down_ref.shape[0]):
            part = part + jnp.dot(
                hidden_rows[:, e * units : (e + 1) * units],
                down_ref[e, :, here],
                preferred_element_type=jnp.float32,
            )
        if got is not None:
            part = part + widen(refs[2][...])
        at = 0
        for n, out_ref in zip(sizes, out_refs):
            out_ref[...] = narrow(part[at : at + n])
            at += n

    specs = [
        pl.BlockSpec((total, inner), lambda n: (block, 0)),
        pl.BlockSpec(memory_space=pltpu.VMEM),
    ]
    operands = [hidden, down]
    if got is not None:
        specs.append(pl.BlockSpec((total, tile), lambda n: (0, n)))
        operands.append(got)
    return pl.pallas_call(
        kernel,
        grid=(steps,),
        in_specs=specs,
        out_specs=[pl.BlockSpec((n, tile), lambda n: (0, n)) for n in sizes],
        out_shape=[jax.ShapeDtypeStruct((n, width), jnp.bfloat16) for n in sizes],
        compiler_params=pltpu.CompilerParams(vmem_limit_bytes=vmem_share),
        cost_estimate=pl.CostEstimate(
            flops=2 * total * inner * width,
            transcendentals=0,
            bytes_accessed=2 * inner * width + 4 * total * width,
        ),
        name="outputs",
    )(*operands)


def attention(q_latent, q_rope, cache_latent, cache_rope, cache_len):
    scores = (
        jnp.einsum("ihl,itl->iht", q_latent, cache_latent, preferred_element_type=jnp.float32)
        + jnp.einsum("ihr,itr->iht", q_rope, cache_rope, preferred_element_type=jnp.float32)
    ) * score_scale
    valid_mask = (
        jnp.arange(cache_latent.shape[1], dtype=jnp.int32)[None, None, :] < cache_len[:, None, None]
    )
    scores = jnp.where(valid_mask, scores, -1e30)
    top_score = jnp.max(scores, axis=-1, keepdims=True)
    exponent = jnp.where(valid_mask, jnp.exp(scores - top_score), 0.0)
    attn_weights = (exponent / jnp.sum(exponent, axis=-1, keepdims=True)).astype(jnp.bfloat16)
    return jnp.einsum(
        "iht,itl->ihl", attn_weights, cache_latent, preferred_element_type=jnp.float32
    ).astype(jnp.bfloat16)


def layer(
    q_latent,
    q_rope,
    cache_latent,
    cache_rope,
    cache_len,
    stream,
    norm_gain,
    expert_ids,
    route_weights,
    w_gate,
    w_up,
    w_down,
):
    row_count, _ = stream.shape
    local_count = w_gate.shape[0]
    first_expert = (lax.axis_index(EP) * local_count).astype(jnp.int32).reshape(1)
    stream_f = widen(stream)
    payload = prepare(stream, norm_gain, expert_ids, route_weights)

    line = jnp.concatenate(spread_direct(payload, 0))
    size = line.shape[0]
    half = size // 2
    near_rows = 3 * size
    near_half = near_rows // 2
    block = 4 * size

    line_behind = move(line, 1, 1)
    line_ahead = move(line, 1, -1)
    line_far_a = move(line_behind[:half], 1, 1)
    line_far_b = move(line_ahead[half:], 1, -1)
    own_a = pack([line, line_behind, line_ahead])
    behind_a = move(own_a, 2, 1)
    ahead_a = move(own_a, 2, -1)
    own_b = pack([line_far_a, line_far_b])
    behind_b = move(own_b, 2, 1)
    ahead_b = move(own_b, 2, -1)
    own_a2 = swap(own_a)
    own_b2 = swap(own_b)
    hid_own, w_gate, w_up, down = first_hidden(
        [own_a, own_b, own_a2, own_b2], w_gate, w_up, w_down, first_expert
    )
    far_wide_a = move(behind_a[:near_half], 2, 1)
    far_wide_b = move(ahead_a[near_half:], 2, -1)
    behind_a2 = swap(behind_a)
    ahead_a2 = swap(ahead_a)
    far_slim_a = move(behind_b[:half], 2, 1)
    far_slim_b = move(ahead_b[half:], 2, -1)
    behind_b2 = swap(behind_b)
    ahead_b2 = swap(ahead_b)
    hid_near = hidden_of([behind_a, behind_b, ahead_a, ahead_b], w_gate, w_up, first_expert)
    behind_a2, hid_near = after((behind_a2, hid_near))
    hid_near_2 = hidden_of([behind_a2, behind_b2, ahead_a2, ahead_b2], w_gate, w_up, first_expert)
    far = [far_wide_a, far_slim_a, far_wide_b, far_slim_b]
    far_2 = [swap(f) for f in far]
    *far_2, hid_near_2 = after((*far_2, hid_near_2))
    hid_far = hidden_of(far + far_2, w_gate, w_up, first_expert)
    (far_part,) = outputs_of(hid_far, 1, [block], down)
    far_got = swap(far_part)
    hid_near_2, far_part = after((hid_near_2, far_part))
    (near_2,) = outputs_of(hid_near_2, 0, [2 * block], down)
    hid_far, near_2 = after((hid_far, near_2))
    near_got = swap(near_2)
    far_a, far_b = outputs_of(hid_far, 0, [block // 2, block // 2], down, far_got)

    via_a = move(far_a, 2, -1)
    via_b = move(far_b, 2, 1)
    pieces = [near_half, near_half, size]
    behind_1, behind_2, behind_b, ahead_1, ahead_2, ahead_b = outputs_of(
        hid_near, 0, pieces + pieces, down, near_got
    )
    even_got_a = move(behind_2, 2, -1)
    even_got_b = move(ahead_1, 2, 1)
    (own_2,) = outputs_of(hid_own, 1, [block], down)
    own_got = swap(own_2)
    mine_1, mine_2, mine_b = outputs_of(hid_own, 0, pieces, down, own_got)
    slim_got_a = move(merge(behind_b, via_a, 0, near_half, half), 2, -1)
    slim_got_b = move(merge(ahead_b, via_b, half, near_half, half), 2, 1)
    odd_got_a = move(merge(behind_1, via_a, 0, 0, near_half), 2, -1)
    odd_got_b = move(merge(ahead_2, via_b, 0, 0, near_half), 2, 1)
    slim = narrow(widen(mine_b) + widen(slim_got_a) + widen(slim_got_b))
    line_via_a = move(slim[:half], 1, -1)
    line_via_b = move(slim[half:], 1, 1)
    own_line, line_b, line_a = settle(
        [mine_1, odd_got_a, even_got_b], [mine_2, even_got_a, odd_got_b], line_via_a, line_via_b
    )
    line_got_a = move(line_b, 1, -1)
    line_got_b = move(line_a, 1, 1)
    line_sum = narrow(widen(own_line) + widen(line_got_a) + widen(line_got_b))
    expert_sum = fold_direct(
        line_sum[:row_count],
        line_sum[row_count : 2 * row_count],
        line_sum[2 * row_count : 3 * row_count],
        line_sum[3 * row_count :],
        0,
    )
    layer_out = narrow(stream_f + expert_sum)
    attn_latent = attention(q_latent, q_rope, cache_latent, cache_rope, cache_len)
    return (attn_latent, layer_out)


def solution(mesh):
    sizes = mesh.shape
    torus = Mesh(mesh.devices.reshape(sizes["rep"], 4, 4, 2), TORUS)
    return jax.shard_map(
        layer,
        mesh=torus,
        in_specs=(
            P(TORUS, None, None),
            P(TORUS, None, None),
            P(TORUS, None, None),
            P(TORUS, None, None),
            P(TORUS),
            P(TORUS, None),
            P(),
            P(TORUS, None),
            P(TORUS, None),
            P(EP, None, "rep"),
            P(EP, None, "rep"),
            P(EP, "rep", None),
        ),
        out_specs=(P(TORUS, None, None), P(TORUS, None)),
        check_vma=False,
    )
```

```python
import jax
import jax.numpy as jnp
from jax import lax
from jax.experimental import pallas as pl
from jax.experimental.pallas import tpu as pltpu
from jax.sharding import Mesh
from jax.sharding import PartitionSpec as P


TORUS = ("rep", "ep_0", "ep_1", "ep_2")
EP = ("ep_0", "ep_1", "ep_2")


score_scale = 192.0 ** (-0.5)
norm_eps = 1e-06
meta_lanes = 128
vmem_share = 12 << 20

PHASE_AXES = ((2, 1, 0), (0, 2, 1))


def torus_pairs(phase, step):
    sizes = [lax.axis_size(a) for a in TORUS]
    pairs = []
    for src in range(sizes[0] * sizes[1] * sizes[2] * sizes[3]):
        rest, core = divmod(src, sizes[3])
        rest, z = divmod(rest, sizes[2])
        x, y = divmod(rest, sizes[1])
        at = [x, y, z]
        axis = PHASE_AXES[core][phase]
        at[axis] = (at[axis] + step) % sizes[axis]
        pairs.append((src, ((at[0] * sizes[1] + at[1]) * sizes[2] + at[2]) * sizes[3] + core))
    return pairs


def move(block, phase, step):
    return lax.ppermute(block, TORUS, torus_pairs(phase, step))


def swap(block):
    return lax.ppermute(block, "ep_2", [(0, 1), (1, 0)])


def after(values):
    return lax.optimization_barrier(values)


def widen(block):
    return block.astype(jnp.float32)


def narrow(block):
    return block.astype(jnp.bfloat16)


def spread_direct(block, phase):
    return [block, move(block, phase, 1), move(block, phase, -1), move(block, phase, 2)]


def fold_direct(own, behind, ahead, across, phase):
    got = [move(behind, phase, -1), move(ahead, phase, 1), move(across, phase, 2)]
    return widen(own) + widen(got[0]) + widen(got[1]) + widen(got[2])


def pack(blocks):
    count = len(blocks)
    sizes = [b.shape[0] for b in blocks]

    def kernel(*refs):
        out_ref = refs[-1]
        at = 0
        for ref, n in zip(refs[:count], sizes):
            out_ref[at : at + n] = ref[...]
            at += n

    return pl.pallas_call(
        kernel,
        in_specs=[pl.BlockSpec(memory_space=pltpu.VMEM)] * count,
        out_shape=jax.ShapeDtypeStruct((sum(sizes), blocks[0].shape[1]), blocks[0].dtype),
        compiler_params=pltpu.CompilerParams(vmem_limit_bytes=vmem_share),
        name="pack",
    )(*blocks)


def merge(block, via, at, via_at, count):
    rows = block.shape[0]

    def kernel(block_ref, via_ref, out_ref):
        if at:
            out_ref[:at] = block_ref[:at]
        added = widen(block_ref[at : at + count]) + widen(via_ref[via_at : via_at + count])
        out_ref[at : at + count] = narrow(added)
        if at + count < rows:
            out_ref[at + count :] = block_ref[at + count :]

    return pl.pallas_call(
        kernel,
        out_shape=jax.ShapeDtypeStruct(block.shape, block.dtype),
        compiler_params=pltpu.CompilerParams(vmem_limit_bytes=vmem_share),
        name="merge",
    )(block, via)


def settle(upper, lower, via_a, via_b):
    half, width = via_a.shape
    size = 2 * half

    def kernel(*refs):
        top = sum(widen(r[...]) for r in refs[:3])
        bottom = sum(widen(r[...]) for r in refs[3:6])
        first_ref, second_ref, third_ref = refs[8:]
        first_ref[...] = narrow(top[:size])
        second_ref[:half] = narrow(top[size:] + widen(refs[6][...]))
        second_ref[half:] = narrow(bottom[:half])
        third_ref[:half] = narrow(bottom[half:size])
        third_ref[half:] = narrow(bottom[size:] + widen(refs[7][...]))

    return pl.pallas_call(
        kernel,
        out_shape=[jax.ShapeDtypeStruct((size, width), via_a.dtype)] * 3,
        compiler_params=pltpu.CompilerParams(vmem_limit_bytes=vmem_share + (8 << 20)),
        name="settle",
    )(*upper, *lower, via_a, via_b)


def prepare(stream, norm_gain, expert_ids, route_weights):
    row_count, width = stream.shape

    def kernel(stream_ref, gain_ref, ids_ref, weights_ref, out_ref):
        rows = widen(stream_ref[...])
        scale = lax.rsqrt(jnp.mean(rows * rows, axis=-1, keepdims=True) + norm_eps)
        out_ref[:, :width] = narrow(rows * scale * gain_ref[...])
        ids = ids_ref[...]
        weights = widen(weights_ref[...])
        lane = lax.broadcasted_iota(jnp.int32, (row_count, meta_lanes), 1)
        table = jnp.zeros((row_count, meta_lanes), jnp.float32)
        for k in range(ids.shape[1]):
            table = jnp.where(lane == ids[:, k : k + 1], weights[:, k : k + 1], table)
        out_ref[:, width:] = narrow(table)

    return pl.pallas_call(
        kernel,
        out_shape=jax.ShapeDtypeStruct((row_count, width + meta_lanes), jnp.bfloat16),
        name="prepare",
    )(stream, norm_gain.reshape(1, -1), expert_ids, route_weights)


def finish(acc_ref, meta, first, out_ref, local_count, units):
    lane = lax.broadcasted_iota(jnp.int32, meta.shape, 1)
    for e in range(local_count):
        mine = jnp.where(lane == first + e, widen(meta), 0.0)
        share = jnp.sum(mine, axis=1, keepdims=True)
        act = jax.nn.silu(acc_ref[2 * e]) * acc_ref[2 * e + 1] * share
        out_ref[:, e * units : (e + 1) * units] = narrow(act)


def first_hidden(blocks, w_gate, w_up, w_down, first_expert):
    local_count, width, units = w_gate.shape
    steps = 7
    tile = width // steps
    total = sum(b.shape[0] for b in blocks)
    count = len(blocks)

    def kernel(first_ref, *refs):
        rows_refs = refs[:count]
        sources = refs[count : count + 3]
        out_ref, gate_ref, up_ref, down_ref, acc_ref, sems, down_sem = refs[count + 3 :]

        def piece(k, which):
            here = pl.ds(k * tile, tile)
            target = (gate_ref, up_ref)[which]
            return pltpu.make_async_copy(
                sources[which].at[:, here, :], target.at[:, here, :], sems.at[k, which]
            )

        for k in range(steps):
            piece(k, 0).start()
            piece(k, 1).start()
        last = pltpu.make_async_copy(sources[2], down_ref, down_sem)
        last.start()
        for k in range(steps):
            here = slice(k * tile, (k + 1) * tile)
            rows = jnp.concatenate([r[:, here] for r in rows_refs], axis=0)
            for which, ref in enumerate((gate_ref, up_ref)):
                piece(k, which).wait()
                for e in range(local_count):
                    part = jnp.dot(rows, ref[e, here, :], preferred_element_type=jnp.float32)
                    if k:
                        part = part + acc_ref[2 * e + which]
                    acc_ref[2 * e + which] = part
        meta = jnp.concatenate([r[:, width:] for r in rows_refs], axis=0)
        finish(acc_ref, meta, first_ref[0], out_ref, local_count, units)
        last.wait()

    weights = (w_gate, w_up, w_down)
    return pl.pallas_call(
        kernel,
        in_specs=[pl.BlockSpec(memory_space=pltpu.SMEM)]
        + [pl.BlockSpec(memory_space=pltpu.VMEM)] * count
        + [pl.BlockSpec(memory_space=pltpu.HBM)] * 3,
        out_specs=[pl.BlockSpec(memory_space=pltpu.VMEM)] * 4,
        out_shape=[jax.ShapeDtypeStruct((total, local_count * units), jnp.bfloat16)]
        + [pltpu.VMEM(w.shape, w.dtype) for w in weights],
        scratch_shapes=[
            pltpu.VMEM((2 * local_count, total, units), jnp.float32),
            pltpu.SemaphoreType.DMA((steps, 2)),
            pltpu.SemaphoreType.DMA,
        ],
        compiler_params=pltpu.CompilerParams(vmem_limit_bytes=vmem_share + (4 << 20)),
        cost_estimate=pl.CostEstimate(
            flops=4 * total * width * units * local_count,
            transcendentals=total * units * local_count,
            bytes_accessed=6 * width * units * local_count,
        ),
        name="first_hidden",
    )(
        first_expert,
        *blocks,
        *[pltpu.with_memory_space_constraint(w, pltpu.HBM) for w in weights],
    )


def hidden_of(blocks, w_gate, w_up, first_expert):
    local_count, width, units = w_gate.shape
    steps = 1
    tile = width // steps
    sizes = [b.shape[0] for b in blocks]
    total = sum(sizes)
    count = len(blocks)

    def kernel(first_ref, *refs):
        rows_refs, meta_refs = refs[:count], refs[count : 2 * count]
        gate_ref, up_ref, out_ref, acc_ref = refs[2 * count :]
        step = pl.program_id(0)

        @pl.when(step == 0)
        def _():
            acc_ref[...] = jnp.zeros_like(acc_ref)

        rows = jnp.concatenate([r[...] for r in rows_refs], axis=0)
        for e in range(local_count):
            gate = gate_ref[e, pl.ds(step * tile, tile), :]
            up = up_ref[e, pl.ds(step * tile, tile), :]
            acc_ref[2 * e] += jnp.dot(rows, gate, preferred_element_type=jnp.float32)
            acc_ref[2 * e + 1] += jnp.dot(rows, up, preferred_element_type=jnp.float32)

        @pl.when(step == steps - 1)
        def _():
            meta = jnp.concatenate([r[...] for r in meta_refs], axis=0)
            finish(acc_ref, meta, first_ref[0], out_ref, local_count, units)

    return pl.pallas_call(
        kernel,
        grid=(steps,),
        in_specs=[pl.BlockSpec(memory_space=pltpu.SMEM)]
        + [pl.BlockSpec((n, tile), lambda k: (0, k)) for n in sizes]
        + [pl.BlockSpec((n, meta_lanes), lambda k: (0, width // meta_lanes)) for n in sizes]
        + [pl.BlockSpec(memory_space=pltpu.VMEM)] * 2,
        out_specs=pl.BlockSpec((total, local_count * units), lambda k: (0, 0)),
        out_shape=jax.ShapeDtypeStruct((total, local_count * units), jnp.bfloat16),
        scratch_shapes=[pltpu.VMEM((2 * local_count, total, units), jnp.float32)],
        compiler_params=pltpu.CompilerParams(vmem_limit_bytes=vmem_share),
        cost_estimate=pl.CostEstimate(
            flops=4 * total * width * units * local_count,
            transcendentals=total * units * local_count,
            bytes_accessed=4 * width * units * local_count + 2 * total * width,
        ),
        name="hidden",
    )(first_expert, *blocks, *blocks, w_gate, w_up)


def outputs_of(hidden, block, sizes, down, got=None):
    width = down.shape[2]
    inner = hidden.shape[1]
    steps = 2
    tile = width // steps
    total = sum(sizes)

    def kernel(*refs):
        hidden_ref, down_ref = refs[:2]
        out_refs = refs[-len(sizes) :]
        here = pl.ds(pl.multiple_of(pl.program_id(0) * tile, 128), tile)
        hidden_rows = hidden_ref[...]
        units = inner // down_ref.shape[0]
        part = jnp.zeros((total, tile), jnp.float32)
        for e in range(down_ref.shape[0]):
            part = part + jnp.dot(
                hidden_rows[:, e * units : (e + 1) * units],
                down_ref[e, :, here],
                preferred_element_type=jnp.float32,
            )
        if got is not None:
            part = part + widen(refs[2][...])
        at = 0
        for n, out_ref in zip(sizes, out_refs):
            out_ref[...] = narrow(part[at : at + n])
            at += n

    specs = [
        pl.BlockSpec((total, inner), lambda n: (block, 0)),
        pl.BlockSpec(memory_space=pltpu.VMEM),
    ]
    operands = [hidden, down]
    if got is not None:
        specs.append(pl.BlockSpec((total, tile), lambda n: (0, n)))
        operands.append(got)
    return pl.pallas_call(
        kernel,
        grid=(steps,),
        in_specs=specs,
        out_specs=[pl.BlockSpec((n, tile), lambda n: (0, n)) for n in sizes],
        out_shape=[jax.ShapeDtypeStruct((n, width), jnp.bfloat16) for n in sizes],
        compiler_params=pltpu.CompilerParams(vmem_limit_bytes=vmem_share),
        cost_estimate=pl.CostEstimate(
            flops=2 * total * inner * width,
            transcendentals=0,
            bytes_accessed=2 * inner * width + 4 * total * width,
        ),
        name="outputs",
    )(*operands)


def attention(q_latent, q_rope, cache_latent, cache_rope, cache_len):
    scores = (
        jnp.einsum("ihl,itl->iht", q_latent, cache_latent, preferred_element_type=jnp.float32)
        + jnp.einsum("ihr,itr->iht", q_rope, cache_rope, preferred_element_type=jnp.float32)
    ) * score_scale
    valid_mask = (
        jnp.arange(cache_latent.shape[1], dtype=jnp.int32)[None, None, :] < cache_len[:, None, None]
    )
    scores = jnp.where(valid_mask, scores, -1e30)
    top_score = jnp.max(scores, axis=-1, keepdims=True)
    exponent = jnp.where(valid_mask, jnp.exp(scores - top_score), 0.0)
    attn_weights = (exponent / jnp.sum(exponent, axis=-1, keepdims=True)).astype(jnp.bfloat16)
    return jnp.einsum(
        "iht,itl->ihl", attn_weights, cache_latent, preferred_element_type=jnp.float32
    ).astype(jnp.bfloat16)


def layer(
    q_latent,
    q_rope,
    cache_latent,
    cache_rope,
    cache_len,
    stream,
    norm_gain,
    expert_ids,
    route_weights,
    w_gate,
    w_up,
    w_down,
):
    row_count, _ = stream.shape
    local_count = w_gate.shape[0]
    first_expert = (lax.axis_index(EP) * local_count).astype(jnp.int32).reshape(1)
    stream_f = widen(stream)
    payload = prepare(stream, norm_gain, expert_ids, route_weights)

    line = pack(spread_direct(payload, 0))
    size = line.shape[0]
    half = size // 2
    near_rows = 3 * size
    near_half = near_rows // 2
    block = 4 * size

    line_behind = move(line, 1, 1)
    line_ahead = move(line, 1, -1)
    line_far_a = move(line_behind[:half], 1, 1)
    line_far_b = move(line_ahead[half:], 1, -1)
    own_a = pack([line, line_behind, line_ahead])
    behind_a = move(own_a, 2, 1)
    ahead_a = move(own_a, 2, -1)
    own_b = pack([line_far_a, line_far_b])
    behind_b = move(own_b, 2, 1)
    ahead_b = move(own_b, 2, -1)
    own_a2 = swap(own_a)
    own_b2 = swap(own_b)
    hid_own, w_gate, w_up, down = first_hidden(
        [own_a, own_b, own_a2, own_b2], w_gate, w_up, w_down, first_expert
    )
    far_wide_a = move(behind_a[:near_half], 2, 1)
    far_wide_b = move(ahead_a[near_half:], 2, -1)
    behind_a2 = swap(behind_a)
    ahead_a2 = swap(ahead_a)
    far_slim_a = move(behind_b[:half], 2, 1)
    far_slim_b = move(ahead_b[half:], 2, -1)
    behind_b2 = swap(behind_b)
    ahead_b2 = swap(ahead_b)
    hid_near = hidden_of([behind_a, behind_b, ahead_a, ahead_b], w_gate, w_up, first_expert)
    behind_a2, hid_near = after((behind_a2, hid_near))
    hid_near_2 = hidden_of([behind_a2, behind_b2, ahead_a2, ahead_b2], w_gate, w_up, first_expert)
    far = [far_wide_a, far_slim_a, far_wide_b, far_slim_b]
    far_2 = [swap(f) for f in far]
    *far_2, hid_near_2 = after((*far_2, hid_near_2))
    hid_far = hidden_of(far + far_2, w_gate, w_up, first_expert)
    (far_part,) = outputs_of(hid_far, 1, [block], down)
    far_got = swap(far_part)
    hid_near_2, far_part = after((hid_near_2, far_part))
    (near_2,) = outputs_of(hid_near_2, 0, [2 * block], down)
    hid_far, near_2 = after((hid_far, near_2))
    near_got = swap(near_2)
    far_a, far_b = outputs_of(hid_far, 0, [block // 2, block // 2], down, far_got)

    via_a = move(far_a, 2, -1)
    via_b = move(far_b, 2, 1)
    pieces = [near_half, near_half, size]
    behind_1, behind_2, behind_b, ahead_1, ahead_2, ahead_b = outputs_of(
        hid_near, 0, pieces + pieces, down, near_got
    )
    even_got_a = move(behind_2, 2, -1)
    even_got_b = move(ahead_1, 2, 1)
    (own_2,) = outputs_of(hid_own, 1, [block], down)
    own_got = swap(own_2)
    mine_1, mine_2, mine_b = outputs_of(hid_own, 0, pieces, down, own_got)
    slim_got_a = move(merge(behind_b, via_a, 0, near_half, half), 2, -1)
    slim_got_b = move(merge(ahead_b, via_b, half, near_half, half), 2, 1)
    odd_got_a = move(merge(behind_1, via_a, 0, 0, near_half), 2, -1)
    odd_got_b = move(merge(ahead_2, via_b, 0, 0, near_half), 2, 1)
    slim = narrow(widen(mine_b) + widen(slim_got_a) + widen(slim_got_b))
    line_via_a = move(slim[:half], 1, -1)
    line_via_b = move(slim[half:], 1, 1)
    own_line, line_b, line_a = settle(
        [mine_1, odd_got_a, even_got_b], [mine_2, even_got_a, odd_got_b], line_via_a, line_via_b
    )
    line_got_a = move(line_b, 1, -1)
    line_got_b = move(line_a, 1, 1)
    line_sum = narrow(widen(own_line) + widen(line_got_a) + widen(line_got_b))
    expert_sum = fold_direct(
        line_sum[:row_count],
        line_sum[row_count : 2 * row_count],
        line_sum[2 * row_count : 3 * row_count],
        line_sum[3 * row_count :],
        0,
    )
    layer_out = narrow(stream_f + expert_sum)
    attn_latent = attention(q_latent, q_rope, cache_latent, cache_rope, cache_len)
    return (attn_latent, layer_out)


def solution(mesh):
    sizes = mesh.shape
    torus = Mesh(mesh.devices.reshape(sizes["rep"], 4, 4, 2), TORUS)
    return jax.shard_map(
        layer,
        mesh=torus,
        in_specs=(
            P(TORUS, None, None),
            P(TORUS, None, None),
            P(TORUS, None, None),
            P(TORUS, None, None),
            P(TORUS),
            P(TORUS, None),
            P(),
            P(TORUS, None),
            P(TORUS, None),
            P(EP, None, "rep"),
            P(EP, None, "rep"),
            P(EP, "rep", None),
        ),
        out_specs=(P(TORUS, None, None), P(TORUS, None)),
        check_vma=False,
    )
```
